32 devices in a mesh: dp: 4 (over y, x), seq: 8 (over z, core).
Axes of the slice: x: 2, y: 2, z: 4, core: 2. Of those that a mesh axis runs over, the one named last changes fastest.
Arguments:
- inputs: bfloat16 [8, 1024, 1280], P('dp', 'seq'), may hold values from -6 to 6
- cotangent: bfloat16 [8, 1024, 1280], P('dp', 'seq'), may hold values from -6 to 6
- w_query: bfloat16 [1280, 1280], P(('dp', 'seq')), may hold values from -0.15625 to 0.15625
- w_key: bfloat16 [1280, 1280], P(('dp', 'seq')), may hold values from -0.15625 to 0.15625
- w_value: bfloat16 [1280, 1280], P(('dp', 'seq')), may hold values from -0.15625 to 0.15625
- w_out: bfloat16 [1280, 1280], P(('dp', 'seq')), may hold values from -1.25 to 1.25
- w_up: bfloat16 [1280, 1280], P(('dp', 'seq')), may hold values from -0.15625 to 0.15625
- w_down: bfloat16 [1280, 1280], P(('dp', 'seq')), may hold values from -0.15625 to 0.15625
- norm_attn: bfloat16 [1280], P(('dp', 'seq')), may hold values from 0.5 to 1.5
- norm_mlp: bfloat16 [1280], P(('dp', 'seq')), may hold values from 0.5 to 1.5
- query_scale: bfloat16 [1280], P(('dp', 'seq')), may hold values from 0 to 1.5
Outputs:
- output: bfloat16 [8, 1024, 1280], P('dp', 'seq')
- input_grad: float32 [8, 1024, 1280], P('dp', 'seq')
- grad_query: float32 [1280, 1280], P(('dp', 'seq'))
- grad_key: float32 [1280, 1280], P(('dp', 'seq'))
- grad_value: float32 [1280, 1280], P(('dp', 'seq'))
- grad_out: float32 [1280, 1280], P(('dp', 'seq'))
- grad_up: float32 [1280, 1280], P(('dp', 'seq'))
- grad_down: float32 [1280, 1280], P(('dp', 'seq'))
- grad_norm_attn: float32 [1280], P(('dp', 'seq'))
- grad_norm_mlp: float32 [1280], P(('dp', 'seq'))
- grad_query_scale: float32 [1280], P(('dp', 'seq'))
The draws below stay inside these ranges and needn't reach their ends.
All inputs are finite; a program needn't handle non-finite values.
Results may differ from the reference program's by a relative error of at most 0.014.
Values may be sent and summed in bfloat16 or wider, within the bound.
No kernel may reach another device: no remote copies, remote signals or barrier semaphores. Data moves between devices by JAX's collectives and lax.ppermute only.
A program may use at most 320 MiB of HBM per device.

```python
import math
import jax
import jax.numpy as jnp
from jax import lax

D = 1280
H = 16
F = 1280
LENGTH = 1024
SEQS = 8


def levels(stream_key, dims, shards, low, high):
    def one(position, shards_of):
        steps = jax.random.uniform(jax.random.fold_in(jax.random.fold_in(stream_key, 6), position), (shards_of,), jnp.float32, low / len(shards), high / len(shards))
        return jnp.repeat(jnp.exp(steps), dims[position] // shards_of).reshape((-1,) + (1,) * (len(dims) - position - 1))

    loudness = one(*shards[0])
    for cut in shards[1:]:
        loudness = loudness * one(*cut)
    return loudness


def bell_draw(rng, extent, spread, bound, shards=(), held_as=jnp.bfloat16):
    array = spread * jax.random.normal(rng, extent, jnp.float32)
    if shards:
        array = array * levels(rng, extent, shards, -0.22, 0.18)
    return jnp.clip(array, -bound, bound).astype(held_as)


def setup_inputs(seed: int = 0) -> dict:
    seeds = jax.random.split(jax.random.key(seed), 12)
    inputs = bell_draw(seeds[0], (SEQS, LENGTH, D), 1.0, 6.0, ((0, 4), (1, 8)))
    cotangent = bell_draw(seeds[1], (SEQS, LENGTH, D), 1.0, 6.0, ((0, 4), (1, 8)))
    w_query = bell_draw(seeds[2], (D, D), D ** -0.5, 0.15625, ((0, 32),))
    w_key = bell_draw(seeds[3], (D, D), D ** -0.5, 0.15625, ((0, 32),))
    w_value = bell_draw(seeds[4], (D, D), D ** -0.5, 0.15625, ((0, 32),))
    w_out = bell_draw(seeds[5], (D, D), (D // 64) ** -0.5, 1.25, ((0, 32),))
    w_up = bell_draw(seeds[6], (D, F), D ** -0.5, 0.15625, ((0, 32),))
    w_down = bell_draw(seeds[7], (F, D), F ** -0.5, 0.15625, ((0, 32),))
    norm_attn = jnp.clip(1.0 + 0.1 * jax.random.normal(seeds[8], (D,), jnp.float32), 0.5, 1.5).astype(jnp.bfloat16)
    norm_mlp = jnp.clip(1.0 + 0.1 * jax.random.normal(seeds[9], (D,), jnp.float32), 0.5, 1.5).astype(jnp.bfloat16)
    query_scale = jnp.clip(1.5 * jax.random.uniform(seeds[10], (D,), jnp.float32) ** levels(seeds[10], (D,), ((0, 32),), -0.2, 0.2), 0.0, 1.5).astype(jnp.bfloat16)
    return dict(inputs=inputs, cotangent=cotangent, w_query=w_query, w_key=w_key, w_value=w_value, w_out=w_out, w_up=w_up, w_down=w_down, norm_attn=norm_attn, norm_mlp=norm_mlp, query_scale=query_scale)


@jax.custom_vjp
def low(v):
    return lax.optimization_barrier(v.astype(jnp.bfloat16)).astype(jnp.float32)

@jax.custom_vjp
def low_back(v):
    return v

def low_keep(v):
    return (low(v), None)

def low_pass(kept, grad):
    return (grad,)

def back_keep(v):
    return (v, None)

def back_low(kept, grad):
    return (low(grad),)
low.defvjp(low_keep, low_pass)
low_back.defvjp(back_keep, back_low)
EPS = 1e-06
SOFT_BASE = 1.442695

def layer(inputs, w_query, w_key, w_value, w_out, w_up, w_down, norm_attn, norm_mlp, query_scale):
    seq_len, model_width = inputs.shape
    head_size = model_width // H
    highest = lax.Precision.HIGHEST
    inv_attn = lax.rsqrt(lax.optimization_barrier(jnp.mean(inputs * inputs, axis=-1, keepdims=True)) + EPS)
    h_attn = low(inputs * inv_attn * norm_attn)
    q_raw = low_back(jnp.dot(h_attn, w_query, precision=highest))
    scale = jax.nn.softplus(query_scale) * (SOFT_BASE / math.sqrt(head_size))
    q_low = low(q_raw * scale)
    k_low = low(low_back(jnp.dot(h_attn, w_key, precision=highest)))
    v_low = low(low_back(jnp.dot(h_attn, w_value, precision=highest)))
    block_rows = min(512, seq_len)
    block_count = seq_len // block_rows
    key_heads = k_low.reshape(seq_len, H, head_size)
    value_heads = v_low.reshape(seq_len, H, head_size)
    key_place = jnp.arange(seq_len, dtype=jnp.int32)

    def one_block(packed):
        query_block, first = packed
        query_heads = query_block.reshape(block_rows, H, head_size)
        scores = low_back(jnp.einsum('qhd,khd->hqk', query_heads, key_heads, precision=highest))
        query_place = first + jnp.arange(block_rows, dtype=jnp.int32)
        allowed = key_place[None, :] <= query_place[:, None]
        probs = jax.nn.softmax(jnp.where(allowed[None], scores, -1e+30), axis=-1)
        mixed = jnp.einsum('hqk,khd->qhd', low(probs), value_heads, precision=highest)
        return mixed.reshape(block_rows, model_width)
    starts = jnp.arange(block_count, dtype=jnp.int32) * block_rows
    mixed = lax.map(jax.checkpoint(one_block), (q_low.reshape(block_count, block_rows, model_width), starts))
    attn_in = low(low_back(mixed.reshape(seq_len, model_width)))
    resid = inputs + low_back(jnp.dot(attn_in, w_out, precision=highest))
    inv_mlp = lax.rsqrt(lax.optimization_barrier(jnp.mean(resid * resid, axis=-1, keepdims=True)) + EPS)
    h_mlp = low(resid * inv_mlp * norm_mlp)
    up_proj = low_back(jnp.dot(h_mlp, w_up, precision=highest))
    activated = low(jax.nn.silu(up_proj))
    return resid + jnp.dot(activated, w_down, precision=highest)

def reference(inputs, cotangent, w_query, w_key, w_value, w_out, w_up, w_down, norm_attn, norm_mlp, query_scale):
    floats = tuple((item.astype(jnp.float32) for item in (w_query, w_key, w_value, w_out, w_up, w_down, norm_attn, norm_mlp, query_scale)))

    def scan_step(totals, packed):
        seq_in, seq_cot = packed
        result, pull = jax.vjp(layer, seq_in, *floats)
        grads = pull(seq_cot)
        summed = tuple((total + grad for total, grad in zip(totals, grads[1:])))
        return (summed, (result.astype(jnp.bfloat16), grads[0]))
    zeros = tuple((jnp.zeros_like(item) for item in floats))
    totals, (results, in_grads) = lax.scan(scan_step, zeros, (inputs.astype(jnp.float32), cotangent.astype(jnp.float32)))
    return (results, in_grads, totals[0], totals[1], totals[2], totals[3], totals[4], totals[5], totals[6], totals[7], totals[8])
```

```python
import functools
import math

import jax
import jax.numpy as jnp
from jax import lax
from jax.experimental import pallas as pl
from jax.experimental.pallas import tpu as pltpu
from jax.sharding import Mesh
from jax.sharding import PartitionSpec as P

H = 16
EPS = 1e-06
SOFT_BASE = 1.442695
BF = jnp.bfloat16
F32 = jnp.float32
NN = (((1,), (0,)), ((), ()))
NT = (((1,), (1,)), ((), ()))
TN = (((0,), (0,)), ((), ()))
DP = ("y", "x")
SEQ = ("z", "c")
ALL = ("y", "x", "z", "c")
BLOCK = 256


def mm(left, right, dims):
    return lax.dot_general(left, right, dims, preferred_element_type=F32)


def forward_kernel(hd, x_ref, gain_ref, w_ref, scale_ref, o_ref, h_ref, kn_ref, vn_ref, qt_ref, kt_ref, ot_ref, lse_ref):
    length = x_ref.shape[0]
    cols = w_ref.shape[0] // 3
    heads = cols // hd
    step = min(BLOCK, length)
    w = w_ref[...]
    gain = gain_ref[...]
    vt_parts = []
    for r in range(0, length, step):
        x = x_ref[r : r + step, :].astype(F32)
        inv = lax.rsqrt(jnp.mean(x * x, axis=-1, keepdims=True) + EPS)
        h = (x * inv * gain).astype(BF)
        h_ref[r : r + step, :] = h
        qkv = mm(w, h, NT)
        q = (qkv[:cols] * scale_ref[...]).astype(BF)
        k = qkv[cols : 2 * cols].astype(BF)
        v = qkv[2 * cols :].astype(BF)
        qt_ref[:, r : r + step] = q
        kt_ref[:, r : r + step] = k
        kn_ref[r : r + step, :] = qkv[cols : 2 * cols].T.astype(BF)
        vn_ref[r : r + step, :] = qkv[2 * cols :].T.astype(BF)
        vt_parts.append(v)
    vt = jnp.concatenate(vt_parts, axis=1)
    zero = jnp.zeros((hd, step), BF)
    causal = lax.broadcasted_iota(jnp.int32, (step, step), 0) <= lax.broadcasted_iota(jnp.int32, (step, step), 1)
    out_block = o_ref.shape[2]
    for r in range(0, length, step):
        n = r + step
        keys = kn_ref[0:n, :]
        outs = []
        for a in range(heads):
            qh = qt_ref[a * hd : (a + 1) * hd, r:n]
            qh = jnp.concatenate([qh if b == a else zero for b in range(heads)], axis=0)
            s = mm(keys, qh, NN)
            tail = jnp.where(causal, s[r:], -1e30)
            s = jnp.concatenate([s[:r], tail], axis=0) if r else tail
            top = jnp.max(s, axis=0, keepdims=True)
            p = jnp.exp(s - top)
            total = jnp.sum(p, axis=0, keepdims=True)
            o = mm(vt[a * hd : (a + 1) * hd, :n], p.astype(BF), NN) / total
            lse_ref[a : a + 1, r:n] = top + jnp.log(total)
            outs.append(o)
        o = jnp.concatenate(outs, axis=0)
        ot_ref[:, r:n] = o
        for b in range(r // out_block, n // out_block):
            o_ref[b] = o[:, b * out_block - r : (b + 1) * out_block - r].astype(BF)


def attention_forward(x, gain, w_t, scale, hd, blocks):
    micro, length, width = x.shape
    cols = w_t.shape[0] // 3
    rows = length // blocks
    step = pl.Squeezed()
    return pl.pallas_call(
        functools.partial(forward_kernel, hd),
        grid=(micro,),
        in_specs=[
            pl.BlockSpec((step, length, width), lambda m: (m, 0, 0)),
            pl.BlockSpec((1, width), lambda m: (0, 0)),
            pl.BlockSpec((3 * cols, width), lambda m: (0, 0)),
            pl.BlockSpec((cols, 1), lambda m: (0, 0)),
        ],
        out_specs=[
            pl.BlockSpec((blocks, cols, rows), lambda m: (0, 0, m)),
            pl.BlockSpec((step, length, width), lambda m: (m, 0, 0)),
            pl.BlockSpec((step, length, cols), lambda m: (m, 0, 0)),
            pl.BlockSpec((step, length, cols), lambda m: (m, 0, 0)),
            pl.BlockSpec((step, cols, length), lambda m: (m, 0, 0)),
            pl.BlockSpec((step, cols, length), lambda m: (m, 0, 0)),
            pl.BlockSpec((step, cols, length), lambda m: (m, 0, 0)),
            pl.BlockSpec((step, 8, length), lambda m: (m, 0, 0)),
        ],
        out_shape=[
            jax.ShapeDtypeStruct((blocks, cols, micro * rows), BF),
            jax.ShapeDtypeStruct((micro, length, width), BF),
            jax.ShapeDtypeStruct((micro, length, cols), BF),
            jax.ShapeDtypeStruct((micro, length, cols), BF),
            jax.ShapeDtypeStruct((micro, cols, length), BF),
            jax.ShapeDtypeStruct((micro, cols, length), BF),
            jax.ShapeDtypeStruct((micro, cols, length), F32),
            jax.ShapeDtypeStruct((micro, 8, length), F32),
        ],
        compiler_params=pltpu.CompilerParams(vmem_limit_bytes=56 << 20),
        name="attention_forward",
    )(x, gain, w_t, scale)


def backward_kernel(hd, do_ref, kn_ref, vn_ref, qt_ref, kt_ref, ot_ref, lse_ref, scale_ref, g_ref, gs_ref, dk_acc, dv_acc):
    blocks, cols, rows = do_ref.shape
    length = blocks * rows
    heads = cols // hd
    step = min(BLOCK, length)
    do = jnp.concatenate([do_ref[b] for b in range(blocks)], axis=1)
    zero = jnp.zeros((hd, step), BF)
    causal = lax.broadcasted_iota(jnp.int32, (step, step), 0) <= lax.broadcasted_iota(jnp.int32, (step, step), 1)
    gs = jnp.zeros((cols, 1), F32)
    for r in range(length - step, -1, -step):
        n = r + step
        keys, values = kn_ref[0:n, :], vn_ref[0:n, :]
        prod = do[:, r:n].astype(F32) * ot_ref[:, r:n]
        dqs = []
        for a in range(heads):
            lo, hi = a * hd, (a + 1) * hd
            qh, doh = qt_ref[lo:hi, r:n], do[lo:hi, r:n]
            q_wide = jnp.concatenate([qh if b == a else zero for b in range(heads)], axis=0)
            do_wide = jnp.concatenate([doh if b == a else zero for b in range(heads)], axis=0)
            delta = jnp.sum(prod[lo:hi], axis=0, keepdims=True)
            s = mm(keys, q_wide, NN) - lse_ref[a : a + 1, r:n]
            tail = jnp.where(causal, s[r:], -1e30)
            s = jnp.concatenate([s[:r], tail], axis=0) if r else tail
            p = jnp.exp(s)
            dp = mm(values, do_wide, NN)
            ds = (p * (dp - delta)).astype(BF)
            p = p.astype(BF)
            dv = mm(doh, p, NT)
            dk = mm(qh, ds, NT)
            if n == length:
                dv_acc[lo:hi, :] = dv
                dk_acc[lo:hi, :] = dk
            else:
                dv_acc[lo:hi, 0:n] += dv
                dk_acc[lo:hi, 0:n] += dk
            dqs.append(mm(kt_ref[lo:hi, 0:n], ds, NN))
        dq = jnp.concatenate(dqs, axis=0)
        gs = gs + jnp.sum(dq * qt_ref[:, r:n].astype(F32), axis=1, keepdims=True)
        dq = (dq * scale_ref[...]).astype(BF)
        for b in range(r // rows, n // rows):
            g_ref[b, 0:cols] = dq[:, b * rows - r : (b + 1) * rows - r]
    for b in range(blocks):
        g_ref[b, cols : 2 * cols] = dk_acc[:, b * rows : (b + 1) * rows].astype(BF)
        g_ref[b, 2 * cols : 3 * cols] = dv_acc[:, b * rows : (b + 1) * rows].astype(BF)
    gs_ref[...] = gs


def attention_backward(do, saved, scale, hd):
    kn, vn, qt, kt, ot, lse = saved
    micro, length, cols = kn.shape
    blocks = do.shape[0]
    rows = length // blocks
    step = pl.Squeezed()
    return pl.pallas_call(
        functools.partial(backward_kernel, hd),
        grid=(micro,),
        in_specs=[
            pl.BlockSpec((blocks, cols, rows), lambda m: (0, 0, m)),
            pl.BlockSpec((step, length, cols), lambda m: (m, 0, 0)),
            pl.BlockSpec((step, length, cols), lambda m: (m, 0, 0)),
            pl.BlockSpec((step, cols, length), lambda m: (m, 0, 0)),
            pl.BlockSpec((step, cols, length), lambda m: (m, 0, 0)),
            pl.BlockSpec((step, cols, length), lambda m: (m, 0, 0)),
            pl.BlockSpec((step, 8, length), lambda m: (m, 0, 0)),
            pl.BlockSpec((cols, 1), lambda m: (0, 0)),
        ],
        out_specs=[
            pl.BlockSpec((blocks, 3 * cols, rows), lambda m: (0, 0, m)),
            pl.BlockSpec((step, cols, 1), lambda m: (m, 0, 0)),
        ],
        out_shape=[
            jax.ShapeDtypeStruct((blocks, 3 * cols, micro * rows), BF),
            jax.ShapeDtypeStruct((micro, cols, 1), F32),
        ],
        scratch_shapes=[pltpu.VMEM((cols, length), F32), pltpu.VMEM((cols, length), F32)],
        compiler_params=pltpu.CompilerParams(vmem_limit_bytes=56 << 20),
        name="attention_backward",
    )(do, kn, vn, qt, kt, ot, lse, scale)


def exchange(value, axes):
    return lax.all_to_all(value, axes, split_axis=0, concat_axis=0, tiled=True)


def head_parallel(inputs, cotangent, w_query, w_key, w_value, w_out, w_up, w_down, norm_attn, norm_mlp, query_scale):
    micro, rows, width = inputs.shape
    n_dp = lax.axis_size(DP)
    n_seq = lax.axis_size(SEQ)
    n_all = n_dp * n_seq
    hd = width // H
    cols = width // n_seq
    shard = w_query.shape[0]
    seq_index = lax.axis_index(SEQ)
    tokens = micro * rows

    x_all = lax.all_gather(inputs, SEQ, axis=1, tiled=True)
    pad = -(3 * shard + 1) % 128 + 1
    pieces = [w.T.reshape(n_seq, cols, shard) for w in (w_query, w_key, w_value)]
    vectors = jnp.concatenate([norm_attn, norm_mlp, query_scale])
    side = jnp.zeros((cols, pad), BF).at[: 3 * shard, 0].set(vectors)
    packed = jnp.concatenate(pieces + [jnp.broadcast_to(side, (n_seq, cols, pad))], axis=2)
    mine = lax.all_gather(exchange(packed, SEQ), DP, axis=0, tiled=True)
    w_t = jnp.concatenate(
        [
            jnp.transpose(mine[:, :, i * shard : (i + 1) * shard], (1, 0, 2)).reshape(cols, width)
            for i in range(3)
        ],
        axis=0,
    )
    vectors = mine[:, : 3 * shard, 3 * shard].astype(F32)
    gain_attn = vectors[:, :shard].reshape(1, width)
    gain_mlp = vectors[:, shard : 2 * shard].reshape(1, width)
    param = lax.dynamic_slice(vectors[:, 2 * shard :].reshape(width, 1), (seq_index * cols, 0), (cols, 1))
    factor = SOFT_BASE / math.sqrt(hd)
    scale = jax.nn.softplus(param) * factor

    def whole(*shards):
        parts = lax.all_gather(jnp.stack(shards), ALL, axis=0, tiled=False)
        return [parts[:, i].reshape(width, width) for i in range(len(shards))]

    full_out, full_up, full_down = whole(w_out, w_up, w_down)
    full_query, full_key, full_value = whole(w_query, w_key, w_value)

    o, h_all, kn, vn, qt, kt, ot, lse = attention_forward(x_all, gain_attn, w_t, scale, hd, n_seq)
    attn_t = exchange(o, SEQ).reshape(width, tokens)

    xf = inputs.reshape(tokens, width).astype(F32)
    dy_low = cotangent.reshape(tokens, width)
    dy = dy_low.astype(F32)
    resid = xf + mm(attn_t, full_out, TN)
    inv_m = lax.rsqrt(jnp.mean(resid * resid, axis=-1, keepdims=True) + EPS)
    normed = resid * inv_m
    h_mlp = (normed * gain_mlp).astype(BF)
    up = mm(h_mlp, full_up, NN)
    sig = jax.nn.sigmoid(up)
    act = (up * sig).astype(BF)
    output = (resid + mm(act, full_down, NN)).astype(BF)
    d_act = mm(dy_low, full_down, NT)
    d_up = (d_act * sig * (1.0 + up * (1.0 - sig))).astype(BF)
    d_hmlp = mm(d_up, full_up, NT)
    g = d_hmlp * gain_mlp
    d_resid = dy + inv_m * (g - normed * jnp.mean(g * normed, axis=-1, keepdims=True))
    dr_low = d_resid.astype(BF)
    d_mixed_t = mm(full_out, dr_low, NT).astype(BF)
    do = exchange(d_mixed_t.reshape(n_seq, cols, tokens), SEQ)

    grads = [mm(attn_t, dr_low, NN), mm(h_mlp, d_up, TN), mm(act, dy_low, TN)]
    grads = jnp.concatenate([g.astype(BF).reshape(n_all, 1, shard, width) for g in grads], axis=1)
    reduced = lax.psum_scatter(grads.reshape(n_all * 3 * shard, width), ALL, scatter_dimension=0, tiled=True)
    reduced = reduced.astype(F32).reshape(3, shard, width)
    grad_out, grad_up, grad_down = reduced[0], reduced[1], reduced[2]

    d_heads, gs = attention_backward(do, (kn, vn, qt, kt, ot, lse), scale, hd)
    d_tokens = exchange(d_heads, SEQ)
    dq_t = d_tokens[:, :cols].reshape(width, tokens)
    dk_t = d_tokens[:, cols : 2 * cols].reshape(width, tokens)
    dv_t = d_tokens[:, 2 * cols :].reshape(width, tokens)
    d_hattn = mm(dq_t, full_query, (((0,), (1,)), ((), ())))
    d_hattn = d_hattn + mm(dk_t, full_key, (((0,), (1,)), ((), ())))
    d_hattn = d_hattn + mm(dv_t, full_value, (((0,), (1,)), ((), ())))
    inv_a = lax.rsqrt(jnp.mean(xf * xf, axis=-1, keepdims=True) + EPS)
    m = xf * inv_a
    e = d_hattn * gain_attn
    input_grad = d_resid + inv_a * (e - m * jnp.mean(e * m, axis=-1, keepdims=True))

    gs = jnp.sum(gs, axis=0) / scale * jax.nn.sigmoid(param) * factor
    h_blocks = h_all.reshape(micro, n_seq, rows, width)
    d_blocks = d_heads.reshape(n_seq, 3 * cols, micro, rows)
    part = jnp.einsum("msrf,scmr->fc", h_blocks, d_blocks, preferred_element_type=F32).astype(BF)
    part = part.reshape(n_dp, width // n_dp, 3 * cols)
    extra = jnp.zeros((n_dp, 16, 3 * cols), BF).at[:, 0, :cols].set(gs[:, 0].astype(BF))
    part = exchange(jnp.concatenate([part, extra], axis=1), DP)
    part = jnp.sum(part.astype(F32), axis=0)
    last = width // n_dp
    part_w = part[:last].astype(BF).reshape(n_seq, shard, 3 * cols)
    part_s = jnp.broadcast_to(part[last : last + 8].astype(BF), (n_seq, 8, 3 * cols))
    part = exchange(jnp.concatenate([part_w, part_s], axis=1), SEQ).astype(F32)
    grad_query, grad_key, grad_value = [
        jnp.transpose(part[:, :shard, i * cols : (i + 1) * cols], (1, 0, 2)).reshape(shard, width) for i in range(3)
    ]
    first = (lax.axis_index(DP) * n_seq + seq_index) * shard
    grad_scale = lax.dynamic_slice(part[:, shard, :cols].reshape(width), (first,), (shard,))
    low = [w.astype(F32) for w in (w_query, w_key, w_value, w_up)]
    grad_gain_attn = (
        jnp.sum(low[0] * grad_query + low[1] * grad_key + low[2] * grad_value, axis=1) / norm_attn.astype(F32)
    )
    grad_gain_mlp = jnp.sum(low[3] * grad_up, axis=1) / norm_mlp.astype(F32)
    return (
        output.reshape(micro, rows, width),
        input_grad.reshape(micro, rows, width),
        grad_query,
        grad_key,
        grad_value,
        grad_out,
        grad_up,
        grad_down,
        grad_gain_attn,
        grad_gain_mlp,
        grad_scale,
    )


def weight_outer(left, right):
    return lax.dot_general(
        left, right, (((0,), (0,)), ((), ())), preferred_element_type=jnp.float32
    )


def times_transpose(left, right):
    return lax.dot_general(
        left, right, (((1,), (1,)), ((), ())), preferred_element_type=jnp.float32
    )


def norm_back(grad, normed, inverse, gain):
    scaled = grad * gain
    inner = jnp.mean(scaled * normed, axis=-1, keepdims=True)
    return (inverse * (scaled - normed * inner), jnp.sum(grad * normed, axis=0))


def attend(q_low, k_low, v_low, first_row, num_heads):
    group_rows, model_width = q_low.shape
    head_size = model_width // num_heads
    query_heads = q_low.reshape(group_rows, num_heads, head_size)
    query_place = first_row + lax.iota(jnp.int32, group_rows)
    start_state = (
        jnp.full((num_heads, group_rows), -1e30, jnp.float32),
        jnp.zeros((num_heads, group_rows), jnp.float32),
        jnp.zeros((group_rows, model_width), jnp.float32),
    )
    key_piece = lax.all_gather(k_low, "seq", axis=0, tiled=True)
    value_piece = lax.all_gather(v_low, "seq", axis=0, tiled=True)
    count = key_piece.shape[0]

    def attend_compute(state):
        best, total, accum = state
        key_heads = key_piece.reshape(count, num_heads, head_size)
        value_heads = value_piece.reshape(count, num_heads, head_size)
        scores = jnp.einsum(
            "qhd,khd->hqk", query_heads, key_heads, preferred_element_type=jnp.float32
        )
        key_place = lax.iota(jnp.int32, count)
        allowed = (key_place[None, :] <= query_place[:, None])[None]
        scores = jnp.where(allowed, scores, -1e30)
        fresh = jnp.maximum(best, jnp.max(scores, axis=2))
        shrink = jnp.exp(best - fresh)
        probs = jnp.where(allowed, jnp.exp(scores - fresh[:, :, None]), 0.0)
        total = jnp.sum(probs, axis=2)
        mixed = jnp.einsum(
            "hqk,khd->qhd",
            probs.astype(jnp.bfloat16),
            value_heads,
            preferred_element_type=jnp.float32,
        )
        factor = jnp.repeat(shrink.T, head_size, axis=1)
        return (fresh, total, accum * factor + mixed.reshape(group_rows, model_width))

    best, total, accum = lax.cond(
        jnp.int32(0) > first_row + group_rows - 1, lambda state: state, attend_compute, start_state
    )
    mixed = accum / jnp.repeat(total.T, head_size, axis=1)
    return (mixed, best + jnp.log(total))


def query_grads(q_low, d_mixed, k_low, v_low, log_total, row_delta, first_row, num_heads):
    group_rows, model_width = q_low.shape
    head_size = model_width // num_heads
    query_heads = q_low.reshape(group_rows, num_heads, head_size)
    grad_heads = d_mixed.reshape(group_rows, num_heads, head_size)
    query_place = first_row + lax.iota(jnp.int32, group_rows)
    empty = jnp.zeros((group_rows, model_width), jnp.float32)
    key_piece = lax.all_gather(k_low, "seq", axis=0, tiled=True)
    value_piece = lax.all_gather(v_low, "seq", axis=0, tiled=True)
    count = key_piece.shape[0]

    def query_compute(accum):
        key_heads = key_piece.reshape(count, num_heads, head_size)
        value_heads = value_piece.reshape(count, num_heads, head_size)
        scores = jnp.einsum(
            "qhd,khd->hqk", query_heads, key_heads, preferred_element_type=jnp.float32
        )
        key_place = lax.iota(jnp.int32, count)
        allowed = (key_place[None, :] <= query_place[:, None])[None]
        probs = jnp.where(allowed, jnp.exp(scores - log_total[:, :, None]), 0.0)
        d_prob = jnp.einsum(
            "qhd,khd->hqk", grad_heads, value_heads, preferred_element_type=jnp.float32
        )
        d_score = (probs * (d_prob - row_delta[:, :, None])).astype(jnp.bfloat16)
        added = jnp.einsum("hqk,khd->qhd", d_score, key_heads, preferred_element_type=jnp.float32)
        return added.reshape(group_rows, model_width)

    return lax.cond(
        jnp.int32(0) > first_row + group_rows - 1, lambda accum: accum, query_compute, empty
    )


def key_grads(k_low, v_low, q_low, d_mixed, total_all, delta_all, first_row, num_heads):
    group_rows, model_width = k_low.shape
    head_size = model_width // num_heads
    key_heads = k_low.reshape(group_rows, num_heads, head_size)
    value_heads = v_low.reshape(group_rows, num_heads, head_size)
    key_place = first_row + lax.iota(jnp.int32, group_rows)
    empty = jnp.zeros((group_rows, model_width), jnp.float32)
    query_piece = lax.all_gather(q_low, "seq", axis=0, tiled=True)
    grad_piece = lax.all_gather(d_mixed, "seq", axis=0, tiled=True)
    count = query_piece.shape[0]

    def key_compute(state):
        query_heads = query_piece.reshape(count, num_heads, head_size)
        grad_heads = grad_piece.reshape(count, num_heads, head_size)
        scores = jnp.einsum(
            "qhd,khd->hqk", query_heads, key_heads, preferred_element_type=jnp.float32
        )
        query_place = lax.iota(jnp.int32, count)
        allowed = (key_place[None, :] <= query_place[:, None])[None]
        probs = jnp.where(allowed, jnp.exp(scores - total_all[:, :, None]), 0.0)
        d_prob = jnp.einsum(
            "qhd,khd->hqk", grad_heads, value_heads, preferred_element_type=jnp.float32
        )
        d_score = (probs * (d_prob - delta_all[:, :, None])).astype(jnp.bfloat16)
        more_values = jnp.einsum(
            "hqk,qhd->khd",
            probs.astype(jnp.bfloat16),
            grad_heads,
            preferred_element_type=jnp.float32,
        )
        more_keys = jnp.einsum(
            "hqk,qhd->khd", d_score, query_heads, preferred_element_type=jnp.float32
        )
        return (
            more_keys.reshape(group_rows, model_width),
            more_values.reshape(group_rows, model_width),
        )

    return lax.cond(
        jnp.int32(0) + count - 1 < first_row, lambda state: state, key_compute, (empty, empty)
    )


def sequence_parallel(
    inputs,
    cotangent,
    w_query,
    w_key,
    w_value,
    w_out,
    w_up,
    w_down,
    norm_attn,
    norm_mlp,
    query_scale,
):
    micro_count, group_rows, model_width = inputs.shape
    num_heads = H
    head_size = model_width // num_heads
    first_row = lax.axis_index("seq") * group_rows
    results = []
    in_grads = []
    totals = None
    for micro_index in range(micro_count):
        gathered = (
            lax.all_gather(w_query, ("dp", "seq"), axis=0, tiled=True),
            lax.all_gather(w_key, ("dp", "seq"), axis=0, tiled=True),
            lax.all_gather(w_value, ("dp", "seq"), axis=0, tiled=True),
            lax.all_gather(w_out, ("dp", "seq"), axis=0, tiled=True),
            lax.all_gather(w_up, ("dp", "seq"), axis=0, tiled=True),
            lax.all_gather(w_down, ("dp", "seq"), axis=0, tiled=True),
            lax.all_gather(norm_attn, ("dp", "seq"), axis=0, tiled=True),
            lax.all_gather(norm_mlp, ("dp", "seq"), axis=0, tiled=True),
            lax.all_gather(query_scale, ("dp", "seq"), axis=0, tiled=True),
        )
        full_query, full_key, full_value, full_out, full_up, full_down = gathered[:6]
        gain_attn = gathered[6].astype(jnp.float32)
        gain_mlp = gathered[7].astype(jnp.float32)
        scale_param = gathered[8].astype(jnp.float32)
        scale = jax.nn.softplus(scale_param) * (SOFT_BASE / math.sqrt(head_size))
        layer_in = inputs[micro_index].astype(jnp.float32)
        inv_attn = lax.rsqrt(jnp.mean(layer_in * layer_in, axis=-1, keepdims=True) + EPS)
        normed_attn = layer_in * inv_attn
        h_attn = (normed_attn * gain_attn).astype(jnp.bfloat16)
        q_raw = jnp.dot(h_attn, full_query, preferred_element_type=jnp.float32)
        q_low = (q_raw * scale).astype(jnp.bfloat16)
        k_low = jnp.dot(h_attn, full_key, preferred_element_type=jnp.float32).astype(jnp.bfloat16)
        v_low = jnp.dot(h_attn, full_value, preferred_element_type=jnp.float32).astype(jnp.bfloat16)
        mixed, log_total = attend(q_low, k_low, v_low, first_row, num_heads)
        attn_in = mixed.astype(jnp.bfloat16)
        resid = layer_in + jnp.dot(attn_in, full_out, preferred_element_type=jnp.float32)
        inv_mlp = lax.rsqrt(jnp.mean(resid * resid, axis=-1, keepdims=True) + EPS)
        normed_mlp = resid * inv_mlp
        h_mlp = (normed_mlp * gain_mlp).astype(jnp.bfloat16)
        up_proj = jnp.dot(h_mlp, full_up, preferred_element_type=jnp.float32)
        activated = jax.nn.silu(up_proj).astype(jnp.bfloat16)
        layer_out = resid + jnp.dot(activated, full_down, preferred_element_type=jnp.float32)
        results.append(layer_out.astype(jnp.bfloat16))
        regathered = (
            lax.all_gather(w_query, ("dp", "seq"), axis=0, tiled=True),
            lax.all_gather(w_key, ("dp", "seq"), axis=0, tiled=True),
            lax.all_gather(w_value, ("dp", "seq"), axis=0, tiled=True),
            lax.all_gather(w_out, ("dp", "seq"), axis=0, tiled=True),
            lax.all_gather(w_up, ("dp", "seq"), axis=0, tiled=True),
            lax.all_gather(w_down, ("dp", "seq"), axis=0, tiled=True),
        )
        back_query, back_key, back_value, back_out, back_up, back_down = regathered
        cotan_rows = cotangent[micro_index]
        cotan_float = cotan_rows.astype(jnp.float32)
        grad_down = weight_outer(activated, cotan_rows)
        d_act = times_transpose(cotan_rows, back_down)
        sigmoid_up = jax.nn.sigmoid(up_proj)
        d_up = (d_act * sigmoid_up * (1.0 + up_proj * (1.0 - sigmoid_up))).astype(jnp.bfloat16)
        grad_up = weight_outer(h_mlp, d_up)
        d_hmlp = times_transpose(d_up, back_up)
        d_norm_mlp, grad_gain_mlp = norm_back(d_hmlp, normed_mlp, inv_mlp, gain_mlp)
        d_resid = cotan_float + d_norm_mlp
        resid_low = d_resid.astype(jnp.bfloat16)
        grad_out = weight_outer(attn_in, resid_low)
        d_mixed = times_transpose(resid_low, back_out).astype(jnp.bfloat16)
        row_delta = jnp.sum(
            (d_mixed.astype(jnp.float32) * mixed).reshape(group_rows, num_heads, head_size), axis=2
        ).T
        total_all, delta_all = (
            lax.all_gather(log_total, "seq", axis=1, tiled=True),
            lax.all_gather(row_delta, "seq", axis=1, tiled=True),
        )
        d_qlow = query_grads(
            q_low, d_mixed, k_low, v_low, log_total, row_delta, first_row, num_heads
        )
        d_keys, d_values = key_grads(
            k_low, v_low, q_low, d_mixed, total_all, delta_all, first_row, num_heads
        )
        keys_low = d_keys.astype(jnp.bfloat16)
        values_low = d_values.astype(jnp.bfloat16)
        d_qraw = (d_qlow * scale).astype(jnp.bfloat16)
        grad_scale = (
            jnp.sum(d_qlow * q_raw, axis=0)
            * jax.nn.sigmoid(scale_param)
            * (SOFT_BASE / math.sqrt(head_size))
        )
        grad_query = weight_outer(h_attn, d_qraw)
        grad_key = weight_outer(h_attn, keys_low)
        grad_value = weight_outer(h_attn, values_low)
        d_hattn = (
            times_transpose(d_qraw, back_query)
            + times_transpose(keys_low, back_key)
            + times_transpose(values_low, back_value)
        )
        d_norm_attn, grad_gain_attn = norm_back(d_hattn, normed_attn, inv_attn, gain_attn)
        in_grads.append(d_resid + d_norm_attn)
        grad_part = (
            grad_query,
            grad_key,
            grad_value,
            grad_out,
            grad_up,
            grad_down,
            grad_gain_attn,
            grad_gain_mlp,
            grad_scale,
        )
        if totals is None:
            totals = tuple(grad_part)
        else:
            totals = tuple((earlier + later for earlier, later in zip(totals, grad_part)))
    totals = (
        lax.psum_scatter(totals[0], ("dp", "seq"), scatter_dimension=0, tiled=True),
        lax.psum_scatter(totals[1], ("dp", "seq"), scatter_dimension=0, tiled=True),
        lax.psum_scatter(totals[2], ("dp", "seq"), scatter_dimension=0, tiled=True),
        lax.psum_scatter(totals[3], ("dp", "seq"), scatter_dimension=0, tiled=True),
        lax.psum_scatter(totals[4], ("dp", "seq"), scatter_dimension=0, tiled=True),
        lax.psum_scatter(totals[5], ("dp", "seq"), scatter_dimension=0, tiled=True),
        lax.psum_scatter(totals[6], ("dp", "seq"), scatter_dimension=0, tiled=True),
        lax.psum_scatter(totals[7], ("dp", "seq"), scatter_dimension=0, tiled=True),
        lax.psum_scatter(totals[8], ("dp", "seq"), scatter_dimension=0, tiled=True),
    )
    return (
        jnp.stack(results),
        jnp.stack(in_grads),
        totals[0],
        totals[1],
        totals[2],
        totals[3],
        totals[4],
        totals[5],
        totals[6],
        totals[7],
        totals[8],
    )


def solution(mesh):
    n_dp, n_seq = mesh.devices.shape
    if H % n_seq:
        axes, inner, over = mesh, sequence_parallel, (("dp",), ("seq",))
    else:
        core = 2 if n_seq % 2 == 0 else 1
        wide = 2 if n_dp % 2 == 0 else 1
        axes = Mesh(mesh.devices.reshape(n_dp // wide, wide, n_seq // core, core), ALL)
        inner, over = head_parallel, (DP, SEQ)
    block = P(*over, None)
    matrix = P(over[0] + over[1], None)
    vector = P(over[0] + over[1])
    placed = (block,) * 2 + (matrix,) * 6 + (vector,) * 3
    return jax.shard_map(inner, mesh=axes, in_specs=placed, out_specs=placed, check_vma=False)
```
